768 devices in a mesh: fsdp: 32 (over z_hi, x, core), dp: 24 (over y, z_lo).
Axes of the slice: x: 4, y: 8, z: 12 (z_hi: 4, z_lo: 3; z = z_hi * 3 + z_lo), core: 2. Of those that a mesh axis runs over, the one named last changes fastest.
Arguments:
- hidden: bfloat16 [24, 8192, 5120], P('dp', 'fsdp'), may hold values from -6 to 6
- queries: bfloat16 [24, 8192, 2560], P('dp', 'fsdp'), may hold values from -100 to 100
- keys: bfloat16 [24, 8192, 512], P('dp', 'fsdp'), may hold values from -4 to 4
- value_weight: bfloat16 [5120, 512], P('fsdp'), may hold values from -0.078125 to 0.078125
- value_head: bfloat16 [2560], replicated, may hold values from -0.8984375 to 0.8984375
- lengths: int32 [24, 32, 4], P('dp', 'fsdp'), may hold values from 1 to 128, 256 in all within a row
- plan: int32 [24, 128], P('dp', 'fsdp'), may hold values from 0 to 127, each once within a row
- targets: float32 [24, 8192], P('dp', 'fsdp'), may hold values from -5 to 5
- loss_mask: int32 [24, 8192], P('dp', 'fsdp'), may hold values 0 or 1
Outputs:
- values: float32 [24, 8192], P('dp', 'fsdp')
- seq_values: float32 [24, 128], P('dp', 'fsdp')
- d_weight: bfloat16 [5120, 512], P('fsdp')
The draws below stay inside these ranges and needn't reach their ends.
Inputs may be any that keep to these rules, and one draw needn't show every extreme that they name: The 4 lengths of a device sum to 256. `plan`: each data group's row names every slot once.
All inputs are finite; a program needn't handle non-finite values. No bound on the sum of `loss_mask` on one device may be relied on, other than what follows from the above.
Results may differ from the reference program's by a relative error of at most 0.02.
Values may be sent and summed in bfloat16 or wider, within the bound.
No kernel may reach another device: no remote copies, remote signals or barrier semaphores. Data moves between devices by JAX's collectives and lax.ppermute only.
A program may use at most 64 MiB of HBM per device.

```python
import math
import jax
import jax.numpy as jnp
import numpy as np
from jax import lax

D = 5120
KVH = 4
QPK = 5
HD = 128
ROWS = 256
SEQ_DEV = 4
QH = 20
KW = 512
TOK_GROUP = 8192
SEQS = 128
TOKENS = 196608
N_FSDP = 32
N_DP = 24


def paired_draw(key):
    key_part = jax.random.fold_in(key, 11)
    query_part = jax.random.fold_in(key, 12)
    keys = jnp.clip(jax.random.normal(key_part, (N_DP, TOK_GROUP, KVH, HD), jnp.float32), -4.0, 4.0)
    queries = jnp.clip(jax.random.normal(query_part, (N_DP, TOK_GROUP, KVH, QPK, HD), jnp.float32), -4.0, 4.0)
    return (queries.reshape(N_DP, TOK_GROUP, KVH * QPK * HD), keys.reshape(N_DP, TOK_GROUP, KVH * HD))


def draw_queries(key, part):
    return paired_draw(key)[0].astype(jnp.bfloat16)


def draw_keys(key, part):
    return paired_draw(key)[1].astype(jnp.bfloat16)


def plant(entries, key, least, largest):
    place = [jax.random.randint(jax.random.fold_in(key, axis), (), 0, length) for axis, length in enumerate(entries.shape)]
    main_axis = entries.shape.index(max(entries.shape))
    beside = place[:main_axis] + [(place[main_axis] + 1) % entries.shape[main_axis]] + place[main_axis + 1:]
    return entries.at[tuple(place)].set(least).at[tuple(beside)].set(largest)


def spiked(array, own_key, source, target, shards_of, factor):
    owner, partner = [(jnp.arange(array.shape[dim]) // (array.shape[dim] // shards_of)).reshape([-1 if axis == dim else 1 for axis in range(array.ndim)]) for dim in (source, target)]
    chosen = jax.random.permutation(own_key, shards_of)[partner]
    strong = (owner == chosen) | (owner == (partner + shards_of // 2) % shards_of)
    return jnp.where(strong, factor * array, array)


def block_levels(own_key, extent, pieces, smallest, largest):
    loudness = 1.0
    for dim, parts in pieces:
        draws = jax.random.uniform(jax.random.fold_in(jax.random.fold_in(own_key, 6), dim), (parts,), jnp.float32, smallest / len(pieces), largest / len(pieces))
        loudness = loudness * jnp.repeat(jnp.exp(draws), extent[dim] // parts).reshape((-1,) + (1,) * (len(extent) - 1 - dim))
    return loudness


def profile(amount, total, bound, skew):
    loads = [(1 << 20) // math.isqrt(rank ** skew) + 1 for rank in range(2, amount + 1)]
    surplus, holding = total - bound - (amount - 1), [1] * (amount - 1)
    while surplus > 0:
        movable = [i for i in range(amount - 1) if holding[i] < bound]
        mass, budget = sum([loads[i] for i in movable]), surplus
        for i in movable:
            extra = min(bound - holding[i], max(1, budget * loads[i] // mass), surplus)
            holding[i] = holding[i] + extra
            surplus = surplus - extra
    return np.array([bound] + holding)


def uneven(rng, amount, total, most, lean):
    if amount == 2:
        one = jax.random.randint(rng, (), max(1, total - most), min(most, total - 1) + 1)
        return jnp.stack([one, total - one])
    sizes = jnp.asarray(profile(amount, total, most, lean), jnp.int32)
    twos = (amount - 1) // 2
    giver, sink = sizes[1:1 + 2 * twos:2], sizes[2:2 + 2 * twos:2]
    margin = jnp.minimum(giver - 1, most - sink)
    moved = jax.random.randint(jax.random.fold_in(rng, 1), (twos,), 0, 1 << 20) % (margin + 1)
    sizes = sizes.at[1:1 + 2 * twos:2].set(giver - moved).at[2:2 + 2 * twos:2].set(sink + moved)
    return sizes[jax.random.permutation(jax.random.fold_in(rng, 2), amount)]


def noise(own_key, dims, deviation, bound, split=(), kind=jnp.bfloat16):
    values = jax.random.normal(own_key, dims, jnp.float32) * deviation
    if len(split) > 0:
        values = block_levels(own_key, dims, split, -0.22, 0.18) * values
    return jnp.clip(values, min=-bound, max=bound).astype(kind)


def bell_draw_with(own_key, shape, scale, reach, pieces, heavy, kind=jnp.bfloat16):
    values = scale * jax.random.normal(own_key, shape, jnp.float32)
    if pieces:
        values = values * block_levels(own_key, shape, pieces, -0.22, 0.18)
    return jnp.clip(spiked(values, jax.random.fold_in(own_key, 3), *heavy), -reach, reach).astype(kind)


def setup_inputs(seed: int = 0) -> dict:
    streams_of = jax.random.split(jax.random.key(seed), 10)
    hidden = bell_draw_with(streams_of[0], (N_DP, TOK_GROUP, D), 1.0, 6.0, ((0, 24), (1, 32)), (1, 2, 32, 2.75))
    queries = draw_queries(jax.random.fold_in(streams_of[9], 71), 0)
    keys = draw_keys(jax.random.fold_in(streams_of[9], 71), 0)
    value_weight = noise(streams_of[3], (D, KW), D ** -0.5, 0.078125, ((0, 32),))
    value_head = noise(streams_of[4], (QH * HD,), 0.15, 0.8984375)
    lengths = jax.vmap(lambda own: uneven(own, SEQ_DEV, ROWS, ROWS // 2, 2))(jax.random.split(streams_of[5], N_DP * N_FSDP)).reshape((N_DP, N_FSDP, SEQ_DEV)).astype(jnp.int32)
    plan = jax.vmap(lambda own: jax.random.permutation(own, SEQS))(jax.random.split(streams_of[6], N_DP)).reshape((N_DP, SEQS)).astype(jnp.int32)
    targets = noise(streams_of[7], (N_DP, TOK_GROUP), 1.0, 5.0, ((0, 24), (1, 32)), jnp.float32)
    loss_mask = plant((jax.random.randint(streams_of[8], (N_DP, TOK_GROUP), 0, 4) < 3).astype(jnp.int32), jax.random.fold_in(streams_of[8], 1), 0, 1)
    return {"hidden": hidden, "queries": queries, "keys": keys, "value_weight": value_weight, "value_head": value_head, "lengths": lengths, "plan": plan, "targets": targets, "loss_mask": loss_mask}


def segment_ids(lengths):
    ends = jnp.cumsum(lengths)
    position = jnp.arange(ROWS, dtype=jnp.int32)
    return lax.optimization_barrier(jnp.sum((position[:, None] >= ends[None, :]).astype(jnp.int32), axis=1))

def block_pass(x_rows, q_rows, k_rows, lengths, target_rows, mask_rows, value_weight, value_head, grad_scale):
    seg = segment_ids(lengths)
    proj = jnp.dot(x_rows, value_weight, preferred_element_type=jnp.float32).astype(jnp.bfloat16)
    q4 = q_rows.reshape(ROWS, KVH, QPK, HD).astype(jnp.float32)
    k3 = k_rows.reshape(ROWS, KVH, HD).astype(jnp.float32)
    v3 = proj.reshape(ROWS, KVH, HD).astype(jnp.float32)
    head3 = value_head.reshape(KVH, QPK, HD).astype(jnp.float32)
    score = jnp.einsum('tgph,sgh->gpts', q4, k3) * (1.0 / math.sqrt(HD))
    position = jnp.arange(ROWS, dtype=jnp.int32)
    allowed = (seg[:, None] == seg[None, :]) & (position[None, :] <= position[:, None])
    score = jnp.where(allowed[None, None], score, -jnp.inf)
    top = lax.optimization_barrier(jnp.max(score, axis=-1, keepdims=True))
    expo = jnp.exp(score - top)
    probs = (expo / lax.optimization_barrier(jnp.sum(expo, axis=-1, keepdims=True))).astype(jnp.bfloat16)
    mixed = jnp.einsum('gpts,sgh->tgph', probs.astype(jnp.float32), v3)
    token_values = jnp.einsum('tgph,gph->t', mixed, head3)
    slot_hits = (seg[:, None] == jnp.arange(SEQ_DEV, dtype=jnp.int32)[None, :]).astype(jnp.float32)
    slot_mean = lax.optimization_barrier(jnp.sum(slot_hits * token_values[:, None], axis=0)) / lengths.astype(jnp.float32)
    resid = jnp.where(mask_rows == 1, token_values - target_rows, 0.0) * grad_scale
    d_mixed = (resid[:, None, None, None] * head3[None]).astype(jnp.bfloat16)
    d_proj = jnp.einsum('gpts,tgph->sgh', probs.astype(jnp.float32), d_mixed.astype(jnp.float32))
    d_proj = d_proj.astype(jnp.bfloat16).reshape(ROWS, KW)
    partial_value = jnp.dot(x_rows.T, d_proj, preferred_element_type=jnp.float32).astype(jnp.bfloat16)
    return (token_values, slot_mean, partial_value)

def reference(hidden, queries, keys, value_weight, value_head, lengths, plan, targets, loss_mask):
    grad_scale = 1.0 / math.sqrt(TOKENS)
    x_all = hidden.reshape(N_DP, N_FSDP, ROWS, D)
    q_all = queries.reshape(N_DP, N_FSDP, ROWS, QH * HD)
    k_all = keys.reshape(N_DP, N_FSDP, ROWS, KW)
    t_all = targets.reshape(N_DP, N_FSDP, ROWS)
    m_all = loss_mask.reshape(N_DP, N_FSDP, ROWS)

    def group(total, batch):

        def member(acc, item):
            token_values, slot_mean, partial_value = block_pass(item[0], item[1], item[2], item[3], item[4], item[5], value_weight, value_head, grad_scale)
            return (acc + lax.optimization_barrier(partial_value).astype(jnp.float32), (token_values, slot_mean))
        acc, outs = lax.scan(member, jnp.zeros((D, KW), jnp.float32), batch)
        rounded = lax.optimization_barrier(acc.astype(jnp.bfloat16))
        return (total + rounded.astype(jnp.float32), outs)
    total, (vals, means) = lax.scan(group, jnp.zeros((D, KW), jnp.float32), (x_all, q_all, k_all, lengths, t_all, m_all))
    values = vals.reshape(N_DP, TOK_GROUP)
    flat_means = means.reshape(N_DP, SEQS)
    seq_values = jnp.take_along_axis(flat_means, plan.astype(jnp.int32), axis=1)
    return (values, seq_values, total.astype(jnp.bfloat16))
```

```python
import functools
import math

import jax
import jax.numpy as jnp
from jax import lax
from jax.experimental import pallas as pl
from jax.experimental.pallas import tpu as pltpu
from jax.sharding import PartitionSpec as P

KVH = 4
QPK = 5
QH = KVH * QPK
HD = 128
SEQ_DEV = 4
GR = 8
HROWS = KVH * GR
PIECE = 160
PROWS = HROWS + 8
TAIL = 32

NT = (((1,), (1,)), ((), ()))
NN = (((1,), (0,)), ((), ()))
TN = (((0,), (0,)), ((), ()))
VMEM = pltpu.CompilerParams(vmem_limit_bytes=24 * 1024 * 1024)


def dot(a, b, dims):
    return lax.dot_general(a, b, dims, preferred_element_type=jnp.float32)


def split(x):
    high = x.astype(jnp.bfloat16)
    return high, (x - high.astype(jnp.float32)).astype(jnp.bfloat16)


def lane_group(rows):
    return lax.broadcasted_iota(jnp.int32, (rows, HD), 1) // TAIL


def turn(x, shift):
    shift = shift % HD
    return x if shift == 0 else pltpu.roll(x, shift, 1)


def head_rows(head_ref, g):
    row = lax.broadcasted_iota(jnp.int32, (GR, HD), 0)
    out = jnp.zeros((GR, HD), jnp.float32)
    for p in range(QPK):
        q = g * QPK + p
        line = head_ref[0:1, q * HD : (q + 1) * HD].astype(jnp.float32)
        out = jnp.where(row == p, jnp.broadcast_to(line, (GR, HD)), out)
    return out


def pack_tail(parts, r):
    group = lane_group(GR)
    tail = jnp.zeros((GR, HD), jnp.float32)
    for g in range(KVH):
        tail = jnp.where(group == g, turn(parts[g], TAIL * (g - r)), tail)
    return tail


def fold_kernel(w_ref, head_ref, out_ref):
    n = out_ref.shape[0]
    mains, tails = [], []
    for g in range(KVH):
        head = head_rows(head_ref, g).astype(jnp.bfloat16)
        cols = slice(g * HD, (g + 1) * HD)
        mains.append(dot(head, w_ref[0:HD, cols], NT))
        tails.append(dot(head, w_ref[PIECE - HD : PIECE, cols], NT))
    packed = jnp.concatenate(mains + [pack_tail(tails, 3)], axis=0).astype(jnp.bfloat16)
    for i in range(n):
        out_ref[i] = packed


def probs_kernel(len_ref, q_ref, k_ref, out_ref, bias_ref):
    rows = k_ref.shape[0]

    @pl.when(pl.program_id(0) == 0)
    def _():
        s = lax.broadcasted_iota(jnp.int32, (rows, rows), 0)
        t = lax.broadcasted_iota(jnp.int32, (rows, rows), 1)
        start = jnp.zeros((rows, rows), jnp.int32)
        end = 0
        for j in range(SEQ_DEV - 1):
            end = end + len_ref[0, j]
            start = jnp.where(t >= end, end, start)
        bias_ref[...] = jnp.where((s <= t) & (s >= start), 0.0, -jnp.inf)

    bias = bias_ref[...]
    scale = math.log2(math.e) / math.sqrt(HD)
    for p in range(QPK):
        score = dot(k_ref[...], q_ref[:, p * HD : (p + 1) * HD], NT) + bias
        top = jnp.max(score, axis=0, keepdims=True)
        expo = jnp.exp2((score - top) * scale)
        total = jnp.sum(expo, axis=0, keepdims=True)
        out_ref[p] = (expo * (1.0 / total)).astype(jnp.bfloat16)


def main_kernel(grad_scale, len_ref, wh_ref, x_ref, p_ref, target_ref, mask_ref, val_ref, out_ref, wht_ref, gt_ref):
    n = wh_ref.shape[0]
    rows = x_ref.shape[0]
    group32, group8 = lane_group(HROWS), lane_group(GR)
    for k in range(n // 4):
        main = [wh_ref[4 * k + r, 0:HROWS, :].astype(jnp.float32) for r in range(4)]
        tail = [wh_ref[4 * k + r, HROWS:PROWS, :].astype(jnp.float32) for r in range(4)]
        for q in range(5):
            tile = turn(main[q], TAIL * q) if q < 4 else None
            if q >= 1:
                r = q - 1
                tails = jnp.concatenate([turn(tail[r], TAIL * (r - g)) for g in range(KVH)], axis=0)
                tile = tails if tile is None else jnp.where(group32 >= q, tile, tails)
                if r >= 1:
                    tile = jnp.where(group32 < r, turn(main[r], TAIL * r), tile)
            j = 5 * k + q
            wht_ref[:, j * HD : (j + 1) * HD] = tile.astype(jnp.bfloat16)
    u = dot(wht_ref[...], x_ref[...], NT)
    u2 = jnp.concatenate(split(u), axis=0)
    row64 = lax.broadcasted_iota(jnp.int32, (2 * HROWS, rows), 0) % HROWS
    zero64 = jnp.zeros((2 * HROWS, rows), jnp.bfloat16)
    acc = jnp.zeros((2 * HROWS, rows), jnp.float32)
    for q in range(QH):
        own = (q // QPK) * GR + q % QPK
        acc = acc + dot(jnp.where(row64 == own, u2, zero64), p_ref[q], NN)
    values = jnp.sum(acc, axis=0, keepdims=True)
    val_ref[...] = values
    pos = lax.broadcasted_iota(jnp.int32, (1, rows), 1)
    row8 = lax.broadcasted_iota(jnp.int32, (GR, HD), 0)
    lane8 = lax.broadcasted_iota(jnp.int32, (GR, HD), 1)
    means = jnp.zeros((GR, HD), jnp.float32)
    begin = 0
    for j in range(SEQ_DEV):
        size = len_ref[0, j]
        hit = (pos >= begin) & (pos < begin + size)
        begin = begin + size
        total = jnp.sum(jnp.where(hit, values, 0.0), axis=1, keepdims=True)
        mean = jnp.broadcast_to(total, (GR, HD)) / size.astype(jnp.float32)
        high = mean.astype(jnp.bfloat16).astype(jnp.float32)
        middle = (mean - high).astype(jnp.bfloat16).astype(jnp.float32)
        low = mean - high - middle
        term = jnp.where(row8 == QPK, high, jnp.where(row8 == QPK + 1, middle, low))
        means = jnp.where((lane8 == j) & (row8 >= QPK), term, means)
    resid = jnp.where(mask_ref[...] == 1, values - target_ref[...], 0.0) * grad_scale
    r_high, r_low = split(resid)
    both = jnp.concatenate(
        [jnp.broadcast_to(r_high, (HROWS, rows)), jnp.broadcast_to(r_low, (HROWS, rows))], axis=0
    )
    acc = jnp.zeros((2 * HROWS, rows), jnp.float32)
    for q in range(QH):
        own = (q // QPK) * GR + q % QPK
        acc = acc + dot(jnp.where(row64 == own, both, zero64), p_ref[q], NT)
    c = acc[0:HROWS] + acc[HROWS:]
    g2 = dot(jnp.concatenate(split(c), axis=0), x_ref[...], NN)
    gt_ref[...] = g2[0:HROWS] + g2[HROWS:]
    for k in range(n // 4):
        tiles = [gt_ref[:, (5 * k + q) * HD : (5 * k + q + 1) * HD] for q in range(5)]
        for r in range(4):
            main = tiles[r]
            if r:
                main = jnp.where(group32 < 4 - r, turn(tiles[r], -TAIL * r), turn(tiles[r + 1], -TAIL * r))
            tail = pack_tail([tiles[r + 1][g * GR : (g + 1) * GR] for g in range(KVH)], r) + means
            out_ref[4 * k + r] = jnp.concatenate([main, tail], axis=0).astype(jnp.bfloat16)


def group_kernel(plan_ref, in_ref, seq_ref, out_ref):
    total = jnp.sum(in_ref[...].astype(jnp.float32), axis=0).astype(jnp.bfloat16)
    for i in range(out_ref.shape[0]):
        out_ref[i] = total
    row8 = lax.broadcasted_iota(jnp.int32, (GR, HD), 0)
    lane8 = lax.broadcasted_iota(jnp.int32, (GR, HD), 1)
    lane = lax.broadcasted_iota(jnp.int32, (1, SEQ_DEV), 1)
    out = jnp.zeros((1, SEQ_DEV), jnp.float32)
    for i in range(SEQ_DEV):
        slot = plan_ref[0, i]
        block = in_ref[lax.div(slot, SEQ_DEV), HROWS:PROWS, :].astype(jnp.float32)
        block = jnp.where((lane8 == lax.rem(slot, SEQ_DEV)) & (row8 >= QPK), block, 0.0)
        mean = jnp.sum(jnp.sum(block, axis=0, keepdims=True), axis=1, keepdims=True)
        out = jnp.where(lane == i, mean, out)
    seq_ref[...] = out


def weight_kernel(head_ref, in_ref, out_ref):
    total = jnp.sum(in_ref[...].astype(jnp.float32), axis=0)
    main = total[0:HROWS]
    tail = jnp.concatenate([turn(total[HROWS:PROWS], -TAIL * g) for g in range(KVH)], axis=0)
    main2 = jnp.concatenate(split(main), axis=0)
    tail2 = jnp.concatenate(split(tail), axis=0)
    for g in range(KVH):
        head = head_rows(head_ref, g).astype(jnp.bfloat16)
        blank = jnp.zeros((GR, HD), jnp.bfloat16)
        block = jnp.concatenate([head if i == g else blank for i in range(KVH)] * 2, axis=0)
        cols = slice(g * HD, (g + 1) * HD)
        out_ref[0:HD, cols] = dot(main2, block, TN).astype(jnp.bfloat16)
        out_ref[HD:PIECE, cols] = dot(tail2, block, TN)[0:TAIL].astype(jnp.bfloat16)


def whole(shape):
    return pl.BlockSpec(shape, lambda: (0,) * len(shape))


def local(hidden, queries, keys, value_weight, value_head, lengths, plan, targets, loss_mask):
    n = lax.axis_size("fsdp")
    groups = lax.axis_size("dp")
    rows, d = hidden.shape[1:]
    grad_scale = 1.0 / math.sqrt(rows * n * groups)
    bf16, f32 = jnp.bfloat16, jnp.float32
    smem = pl.BlockSpec(memory_space=pltpu.SMEM)
    head = value_head.reshape(1, QH * HD)
    own_lengths = lengths.reshape(1, SEQ_DEV)

    folded = pl.pallas_call(
        fold_kernel,
        out_shape=jax.ShapeDtypeStruct((n, PROWS, HD), bf16),
        compiler_params=VMEM,
        name="fold",
    )(value_weight, head)
    every = lax.all_to_all(folded, "fsdp", 0, 0)

    probs = pl.pallas_call(
        probs_kernel,
        grid=(KVH,),
        in_specs=[
            smem,
            pl.BlockSpec((rows, QPK * HD), lambda g: (0, g)),
            pl.BlockSpec((rows, HD), lambda g: (0, g)),
        ],
        out_specs=pl.BlockSpec((QPK, rows, rows), lambda g: (g, 0, 0)),
        out_shape=jax.ShapeDtypeStruct((QH, rows, rows), bf16),
        scratch_shapes=[pltpu.VMEM((rows, rows), f32)],
        compiler_params=VMEM,
        cost_estimate=pl.CostEstimate(
            flops=2 * QH * rows * rows * HD, bytes_accessed=6 * 2**20, transcendentals=QH * rows * rows
        ),
        name="probs",
    )(own_lengths, queries[0], keys[0])

    values, pieces = pl.pallas_call(
        functools.partial(main_kernel, grad_scale),
        in_specs=[smem] + [pl.BlockSpec(memory_space=pltpu.VMEM)] * 5,
        out_shape=[jax.ShapeDtypeStruct((1, rows), f32), jax.ShapeDtypeStruct((n, PROWS, HD), bf16)],
        scratch_shapes=[pltpu.VMEM((HROWS, d), bf16), pltpu.VMEM((HROWS, d), f32)],
        compiler_params=VMEM,
        name="main",
    )(own_lengths, every, hidden[0], probs, targets, loss_mask)
    terms = lax.all_to_all(pieces, "fsdp", 0, 0)

    seq_values, copies = pl.pallas_call(
        group_kernel,
        in_specs=[smem, pl.BlockSpec(memory_space=pltpu.VMEM)],
        out_shape=[jax.ShapeDtypeStruct((1, SEQ_DEV), f32), jax.ShapeDtypeStruct((groups, PROWS, HD), bf16)],
        compiler_params=VMEM,
        name="group",
    )(plan, terms)
    sums = lax.all_to_all(copies, "dp", 0, 0)

    d_weight = pl.pallas_call(
        weight_kernel,
        out_shape=jax.ShapeDtypeStruct(value_weight.shape, bf16),
        compiler_params=VMEM,
        name="weight",
    )(head, sums)
    return values, seq_values, d_weight


def solution(mesh):
    in_specs = (
        P("dp", "fsdp", None),
        P("dp", "fsdp", None),
        P("dp", "fsdp", None),
        P("fsdp", None),
        P(),
        P("dp", "fsdp", None),
        P("dp", "fsdp"),
        P("dp", "fsdp"),
        P("dp", "fsdp"),
    )
    out_specs = (P("dp", "fsdp"), P("dp", "fsdp"), P("fsdp", None))
    return jax.shard_map(local, mesh=mesh, in_specs=in_specs, out_specs=out_specs, check_vma=False)
```

```python
import functools
import math

import jax
import jax.numpy as jnp
from jax import lax
from jax.experimental import pallas as pl
from jax.experimental.pallas import tpu as pltpu
from jax.sharding import Mesh
from jax.sharding import PartitionSpec as P

KVH = 4
QPK = 5
QH = KVH * QPK
HD = 128
SEQ_DEV = 4
AXES = {"zh": 4, "x": 4, "core": 2, "y": 8, "zl": 3}
FSDP = ("zh", "x", "core")
DP = ("y", "zl")
GR = 8
HROWS = KVH * GR
PIECE = 160
PROWS = HROWS + 8
TAIL = 32

NT = (((1,), (1,)), ((), ()))
NN = (((1,), (0,)), ((), ()))
TN = (((0,), (0,)), ((), ()))
VMEM = pltpu.CompilerParams(vmem_limit_bytes=24 * 1024 * 1024)


def dot(a, b, dims):
    return lax.dot_general(a, b, dims, preferred_element_type=jnp.float32)


def split(x):
    high = x.astype(jnp.bfloat16)
    return high, (x - high.astype(jnp.float32)).astype(jnp.bfloat16)


def lane_group(rows):
    return lax.broadcasted_iota(jnp.int32, (rows, HD), 1) // TAIL


def turn(x, shift):
    shift = shift % HD
    return x if shift == 0 else pltpu.roll(x, shift, 1)


def head_rows(head_ref, g):
    row = lax.broadcasted_iota(jnp.int32, (GR, HD), 0)
    out = jnp.zeros((GR, HD), jnp.float32)
    for p in range(QPK):
        q = g * QPK + p
        line = head_ref[0:1, q * HD : (q + 1) * HD].astype(jnp.float32)
        out = jnp.where(row == p, jnp.broadcast_to(line, (GR, HD)), out)
    return out


def pack_tail(parts, r):
    group = lane_group(GR)
    tail = jnp.zeros((GR, HD), jnp.float32)
    for g in range(KVH):
        tail = jnp.where(group == g, turn(parts[g], TAIL * (g - r)), tail)
    return tail


def fold_kernel(w_ref, head_ref, out_ref):
    n = out_ref.shape[0]
    mains, tails = [], []
    for g in range(KVH):
        head = head_rows(head_ref, g).astype(jnp.bfloat16)
        cols = slice(g * HD, (g + 1) * HD)
        mains.append(dot(head, w_ref[0:HD, cols], NT))
        tails.append(dot(head, w_ref[PIECE - HD : PIECE, cols], NT))
    packed = jnp.concatenate(mains + [pack_tail(tails, 3)], axis=0).astype(jnp.bfloat16)
    for i in range(n):
        out_ref[i] = packed


def probs_kernel(len_ref, q_ref, k_ref, out_ref, bias_ref):
    rows = k_ref.shape[0]

    @pl.when(pl.program_id(0) == 0)
    def _():
        s = lax.broadcasted_iota(jnp.int32, (rows, rows), 0)
        t = lax.broadcasted_iota(jnp.int32, (rows, rows), 1)
        start = jnp.zeros((rows, rows), jnp.int32)
        end = 0
        for j in range(SEQ_DEV - 1):
            end = end + len_ref[0, j]
            start = jnp.where(t >= end, end, start)
        bias_ref[...] = jnp.where((s <= t) & (s >= start), 0.0, -jnp.inf)

    bias = bias_ref[...]
    scale = math.log2(math.e) / math.sqrt(HD)
    for p in range(QPK):
        score = dot(k_ref[...], q_ref[:, p * HD : (p + 1) * HD], NT) + bias
        top = jnp.max(score, axis=0, keepdims=True)
        expo = jnp.exp2((score - top) * scale)
        total = jnp.sum(expo, axis=0, keepdims=True)
        out_ref[p] = (expo * (1.0 / total)).astype(jnp.bfloat16)


def main_kernel(grad_scale, len_ref, own_ref, other_ref, x_ref, p_ref, target_ref, mask_ref, val_ref, out_ref, wht_ref, gt_ref):
    n = 2 * own_ref.shape[0]
    across, depth = out_ref.shape[:2]
    rows = x_ref.shape[0]
    group32 = lane_group(HROWS)
    core = lax.axis_index("core")
    place = (lax.axis_index("zh") * AXES["x"] + lax.axis_index("x")) * AXES["core"] + core

    def piece(i, part):
        own, other = own_ref[i // 2, part, :].astype(jnp.float32), other_ref[i // 2, part, :].astype(jnp.float32)
        return jnp.where(core == i % 2, own, other)

    for k in range(n // 4):
        main = [piece(4 * k + r, slice(0, HROWS)) for r in range(4)]
        tail = [piece(4 * k + r, slice(HROWS, PROWS)) for r in range(4)]
        for q in range(5):
            tile = turn(main[q], TAIL * q) if q < 4 else None
            if q >= 1:
                r = q - 1
                tails = jnp.concatenate([turn(tail[r], TAIL * (r - g)) for g in range(KVH)], axis=0)
                tile = tails if tile is None else jnp.where(group32 >= q, tile, tails)
                if r >= 1:
                    tile = jnp.where(group32 < r, turn(main[r], TAIL * r), tile)
            j = 5 * k + q
            wht_ref[:, j * HD : (j + 1) * HD] = tile.astype(jnp.bfloat16)
    u = dot(wht_ref[...], x_ref[...], NT)
    u2 = jnp.concatenate(split(u), axis=0)
    row64 = lax.broadcasted_iota(jnp.int32, (2 * HROWS, rows), 0) % HROWS
    zero64 = jnp.zeros((2 * HROWS, rows), jnp.bfloat16)
    acc = jnp.zeros((2 * HROWS, rows), jnp.float32)
    for q in range(QH):
        own = (q // QPK) * GR + q % QPK
        acc = acc + dot(jnp.where(row64 == own, u2, zero64), p_ref[q], NN)
    values = jnp.sum(acc, axis=0, keepdims=True)
    val_ref[...] = values
    pos = lax.broadcasted_iota(jnp.int32, (1, rows), 1)
    row8 = lax.broadcasted_iota(jnp.int32, (GR, HD), 0)
    lane8 = lax.broadcasted_iota(jnp.int32, (GR, HD), 1)
    means = jnp.zeros((GR, HD), jnp.float32)
    begin = 0
    for j in range(SEQ_DEV):
        size = len_ref[0, j]
        hit = (pos >= begin) & (pos < begin + size)
        begin = begin + size
        total = jnp.sum(jnp.where(hit, values, 0.0), axis=1, keepdims=True)
        mean = jnp.broadcast_to(total, (GR, HD)) / size.astype(jnp.float32)
        high = mean.astype(jnp.bfloat16).astype(jnp.float32)
        middle = (mean - high).astype(jnp.bfloat16).astype(jnp.float32)
        low = mean - high - middle
        term = jnp.where(row8 == QPK, high, jnp.where(row8 == QPK + 1, middle, low))
        means = jnp.where((lane8 == SEQ_DEV * place + j) & (row8 >= QPK), term, means)
    resid = jnp.where(mask_ref[...] == 1, values - target_ref[...], 0.0) * grad_scale
    r_high, r_low = split(resid)
    both = jnp.concatenate(
        [jnp.broadcast_to(r_high, (HROWS, rows)), jnp.broadcast_to(r_low, (HROWS, rows))], axis=0
    )
    acc = jnp.zeros((2 * HROWS, rows), jnp.float32)
    for q in range(QH):
        own = (q // QPK) * GR + q % QPK
        acc = acc + dot(jnp.where(row64 == own, both, zero64), p_ref[q], NT)
    c2 = jnp.concatenate(split(acc[0:HROWS] + acc[HROWS:]), axis=0)
    g2 = dot(c2, x_ref[...], NN)
    gt_ref[...] = g2[0:HROWS] + g2[HROWS:]
    for k in range(n // 4):
        tiles = [gt_ref[:, (5 * k + q) * HD : (5 * k + q + 1) * HD] for q in range(5)]
        for r in range(4):
            main = tiles[r]
            if r:
                main = jnp.where(group32 < 4 - r, turn(tiles[r], -TAIL * r), turn(tiles[r + 1], -TAIL * r))
            tail = pack_tail([tiles[r + 1][g * GR : (g + 1) * GR] for g in range(KVH)], r) + means
            i = 4 * k + r
            out_ref[i % across, i // across] = jnp.concatenate([main, tail], axis=0).astype(jnp.bfloat16)


def line_kernel(in_ref, out_ref):
    low = AXES["zl"]
    for h in range(AXES["zh"]):
        total = jnp.sum(in_ref[:, h].astype(jnp.float32), axis=0).astype(jnp.bfloat16)
        for i in range(low):
            out_ref[h * low + i] = total


def group_kernel(plan_ref, in_ref, seq_ref, out_ref):
    total = jnp.sum(in_ref[...].astype(jnp.float32), axis=0).astype(jnp.bfloat16)
    for i in range(out_ref.shape[0]):
        out_ref[i] = total
    mine = lax.axis_index("zl")
    block = jnp.zeros((GR, HD), jnp.float32)
    for h in range(AXES["zh"]):
        block = block + in_ref[h * AXES["zl"] + mine, HROWS:PROWS, :].astype(jnp.float32)
    row8 = lax.broadcasted_iota(jnp.int32, (GR, HD), 0)
    mean = jnp.sum(jnp.where(row8 >= QPK, block, 0.0), axis=0, keepdims=True)
    slot = lax.broadcasted_iota(jnp.int32, (1, HD), 1)
    lane = lax.broadcasted_iota(jnp.int32, (1, SEQ_DEV), 1)
    out = jnp.zeros((1, SEQ_DEV), jnp.float32)
    for i in range(SEQ_DEV):
        own = jnp.sum(jnp.where(slot == plan_ref[0, i], mean, 0.0), axis=1, keepdims=True)
        out = jnp.where(lane == i, own, out)
    seq_ref[...] = out


def weight_kernel(head_ref, in_ref, out_ref):
    total = jnp.sum(in_ref[...].astype(jnp.float32), axis=0)
    main = total[0:HROWS]
    tail = jnp.concatenate([turn(total[HROWS:PROWS], -TAIL * g) for g in range(KVH)], axis=0)
    main2 = jnp.concatenate(split(main), axis=0)
    tail2 = jnp.concatenate(split(tail), axis=0)
    for g in range(KVH):
        head = head_rows(head_ref, g).astype(jnp.bfloat16)
        blank = jnp.zeros((GR, HD), jnp.bfloat16)
        block = jnp.concatenate([head if i == g else blank for i in range(KVH)] * 2, axis=0)
        cols = slice(g * HD, (g + 1) * HD)
        out_ref[0:HD, cols] = dot(main2, block, TN).astype(jnp.bfloat16)
        out_ref[HD:PIECE, cols] = dot(tail2, block, TN)[0:TAIL].astype(jnp.bfloat16)


def local(hidden, queries, keys, value_weight, value_head, lengths, plan, targets, loss_mask):
    n = math.prod(AXES[a] for a in FSDP)
    groups = math.prod(AXES[a] for a in DP)
    rows, d = hidden.shape[1:]
    grad_scale = 1.0 / math.sqrt(rows * n * groups)
    bf16, f32 = jnp.bfloat16, jnp.float32
    smem = pl.BlockSpec(memory_space=pltpu.SMEM)
    vmem = pl.BlockSpec(memory_space=pltpu.VMEM)
    head = value_head.reshape(1, QH * HD)
    own_lengths = lengths.reshape(1, SEQ_DEV)

    folded = pl.pallas_call(
        fold_kernel,
        out_shape=jax.ShapeDtypeStruct((n // 2, PROWS, HD), bf16),
        compiler_params=VMEM,
        name="fold",
    )(value_weight, head)
    own_core = lax.all_to_all(folded, ("zh", "x"), 0, 0)
    probs = pl.pallas_call(
        probs_kernel,
        grid=(KVH,),
        in_specs=[
            smem,
            pl.BlockSpec((rows, QPK * HD), lambda g: (0, g)),
            pl.BlockSpec((rows, HD), lambda g: (0, g)),
        ],
        out_specs=pl.BlockSpec((QPK, rows, rows), lambda g: (g, 0, 0)),
        out_shape=jax.ShapeDtypeStruct((QH, rows, rows), bf16),
        scratch_shapes=[pltpu.VMEM((rows, rows), f32)],
        compiler_params=VMEM,
        cost_estimate=pl.CostEstimate(
            flops=2 * QH * rows * rows * HD, bytes_accessed=6 * 2**20, transcendentals=QH * rows * rows
        ),
        name="probs",
    )(own_lengths, queries[0], keys[0])

    own_core, probs = lax.optimization_barrier((own_core, probs))
    other_core = lax.ppermute(own_core, "core", [(0, 1), (1, 0)])

    values, pieces = pl.pallas_call(
        functools.partial(main_kernel, grad_scale),
        in_specs=[smem] + [vmem] * 6,
        out_shape=[
            jax.ShapeDtypeStruct((1, rows), f32),
            jax.ShapeDtypeStruct((n // AXES["zh"], AXES["zh"], PROWS, HD), bf16),
        ],
        scratch_shapes=[pltpu.VMEM((HROWS, d), bf16), pltpu.VMEM((HROWS, d), f32)],
        compiler_params=VMEM,
        name="main",
    )(own_lengths, own_core, other_core, hidden[0], probs, targets, loss_mask)
    terms = lax.all_to_all(pieces, ("x", "core"), 0, 0)

    line = pl.pallas_call(
        line_kernel,
        out_shape=jax.ShapeDtypeStruct((AXES["zh"] * AXES["zl"], PROWS, HD), bf16),
        compiler_params=VMEM,
        name="line",
    )(terms)
    lines = lax.all_to_all(line, ("zh", "zl"), 0, 0)

    seq_values, copies = pl.pallas_call(
        group_kernel,
        in_specs=[smem, vmem],
        out_shape=[jax.ShapeDtypeStruct((1, SEQ_DEV), f32), jax.ShapeDtypeStruct((AXES["y"], PROWS, HD), bf16)],
        compiler_params=VMEM,
        name="group",
    )(plan, lines)
    sums = lax.all_to_all(copies, "y", 0, 0)

    d_weight = pl.pallas_call(
        weight_kernel,
        out_shape=jax.ShapeDtypeStruct(value_weight.shape, bf16),
        compiler_params=VMEM,
        name="weight",
    )(head, sums)
    return values, seq_values, d_weight


def solution(mesh):
    fine = Mesh(mesh.devices.reshape(tuple(AXES.values())), tuple(AXES))
    in_specs = (
        P(DP, FSDP, None),
        P(DP, FSDP, None),
        P(DP, FSDP, None),
        P(FSDP, None),
        P(),
        P(DP, FSDP, None),
        P(DP, FSDP),
        P(DP, FSDP),
        P(DP, FSDP),
    )
    out_specs = (P(DP, FSDP), P(DP, FSDP), P(FSDP, None))
    return jax.shard_map(local, mesh=fine, in_specs=in_specs, out_specs=out_specs, check_vma=False)
```

```python
import functools
import math

import jax
import jax.numpy as jnp
from jax import lax
from jax.experimental import pallas as pl
from jax.experimental.pallas import tpu as pltpu
from jax.sharding import Mesh
from jax.sharding import PartitionSpec as P

KVH = 4
QPK = 5
QH = KVH * QPK
HD = 128
SEQ_DEV = 4
AXES = {"zh": 4, "x": 4, "core": 2, "y": 8, "zl": 3}
FSDP = ("zh", "x", "core")
DP = ("y", "zl")
GR = 8
HROWS = KVH * GR
PIECE = 160
PROWS = HROWS + 8
TAIL = 32

NT = (((1,), (1,)), ((), ()))
NN = (((1,), (0,)), ((), ()))
TN = (((0,), (0,)), ((), ()))
VMEM = pltpu.CompilerParams(vmem_limit_bytes=24 * 1024 * 1024)
WIDE = pltpu.CompilerParams(vmem_limit_bytes=60 * 1024 * 1024)


def dot(a, b, dims):
    return lax.dot_general(a, b, dims, preferred_element_type=jnp.float32)


def split(x):
    high = x.astype(jnp.bfloat16)
    return high, (x - high.astype(jnp.float32)).astype(jnp.bfloat16)


def lane_group(rows):
    return lax.broadcasted_iota(jnp.int32, (rows, HD), 1) // TAIL


def turn(x, shift):
    shift = shift % HD
    return x if shift == 0 else pltpu.roll(x, shift, 1)


def head_rows(head_ref, g):
    row = lax.broadcasted_iota(jnp.int32, (GR, HD), 0)
    out = jnp.zeros((GR, HD), jnp.float32)
    for p in range(QPK):
        q = g * QPK + p
        line = head_ref[q * HD : (q + 1) * HD].astype(jnp.float32).reshape(1, HD)
        out = jnp.where(row == p, jnp.broadcast_to(line, (GR, HD)), out)
    return out


def pack_tail(parts, r):
    group = lane_group(GR)
    tail = jnp.zeros((GR, HD), jnp.float32)
    for g in range(KVH):
        tail = jnp.where(group == g, turn(parts[g], TAIL * (g - r)), tail)
    return tail


def fold_kernel(w_ref, head_ref, out_ref):
    n = out_ref.shape[0]
    mains, tails = [], []
    for g in range(KVH):
        head = head_rows(head_ref, g).astype(jnp.bfloat16)
        cols = slice(g * HD, (g + 1) * HD)
        mains.append(dot(head, w_ref[0:HD, cols], NT))
        tails.append(dot(head, w_ref[PIECE - HD : PIECE, cols], NT))
    packed = jnp.concatenate(mains + [pack_tail(tails, 3)], axis=0).astype(jnp.bfloat16)
    for i in range(n):
        out_ref[i] = packed


def probs_kernel(len_ref, q_ref, k_ref, out_ref, share_ref, bias_ref):
    rows = k_ref.shape[0]

    @pl.when(pl.program_id(0) == 0)
    def _():
        s = lax.broadcasted_iota(jnp.int32, (rows, rows), 0)
        t = lax.broadcasted_iota(jnp.int32, (rows, rows), 1)
        start = jnp.zeros((rows, rows), jnp.int32)
        end = 0
        for j in range(SEQ_DEV - 1):
            end = end + len_ref[0, j]
            start = jnp.where(t >= end, end, start)
        bias_ref[...] = jnp.where((s <= t) & (s >= start), 0.0, -jnp.inf)
        row = lax.broadcasted_iota(jnp.int32, (GR, rows), 0)
        pos = lax.broadcasted_iota(jnp.int32, (GR, rows), 1)
        share = jnp.zeros((GR, rows), jnp.float32)
        begin = 0
        for j in range(SEQ_DEV):
            size = len_ref[0, j]
            hit = (row == j) & (pos >= begin) & (pos < begin + size)
            share = jnp.where(hit, 1.0 / (jnp.zeros((GR, rows), jnp.float32) + size.astype(jnp.float32)), share)
            begin = begin + size
        share_ref[...] = share

    bias = bias_ref[...]
    scale = math.log2(math.e) / math.sqrt(HD)
    for p in range(QPK):
        score = dot(k_ref[...], q_ref[:, p * HD : (p + 1) * HD], NT) + bias
        top = jnp.max(score, axis=0, keepdims=True)
        expo = jnp.exp2((score - top) * scale)
        total = jnp.sum(expo, axis=0, keepdims=True)
        out_ref[p] = (expo * (1.0 / total)).astype(jnp.bfloat16)


def main_kernel(
    grad_scale, seen_ref, share_ref, own_ref, other_ref, x_ref, p_ref, target_ref, mask_ref, val_ref, out_ref, wht_ref, gt_ref
):
    n = 2 * own_ref.shape[0]
    across, depth = out_ref.shape[:2]
    rows = x_ref.shape[0]
    group32 = lane_group(HROWS)
    core = lax.axis_index("core")
    place = (lax.axis_index("zh") * AXES["x"] + lax.axis_index("x")) * AXES["core"] + core

    def piece(i, part):
        own, other = own_ref[i // 2, part, :].astype(jnp.float32), other_ref[i // 2, part, :].astype(jnp.float32)
        return jnp.where(core == i % 2, own, other)

    for k in range(n // 4):
        main = [piece(4 * k + r, slice(0, HROWS)) for r in range(4)]
        tail = [piece(4 * k + r, slice(HROWS, PROWS)) for r in range(4)]
        for q in range(5):
            tile = turn(main[q], TAIL * q) if q < 4 else None
            if q >= 1:
                r = q - 1
                tails = jnp.concatenate([turn(tail[r], TAIL * (r - g)) for g in range(KVH)], axis=0)
                tile = tails if tile is None else jnp.where(group32 >= q, tile, tails)
                if r >= 1:
                    tile = jnp.where(group32 < r, turn(main[r], TAIL * r), tile)
            j = 5 * k + q
            wht_ref[:, j * HD : (j + 1) * HD] = tile.astype(jnp.bfloat16)
    u = dot(wht_ref[...], x_ref[...], NT)
    u2 = jnp.concatenate(split(u), axis=0)
    row64 = lax.broadcasted_iota(jnp.int32, (2 * HROWS, rows), 0) % HROWS
    zero64 = jnp.zeros((2 * HROWS, rows), jnp.bfloat16)
    acc = jnp.zeros((2 * HROWS, rows), jnp.float32)
    for q in range(QH):
        own = (q // QPK) * GR + q % QPK
        acc = acc + dot(jnp.where(row64 == own, u2, zero64), p_ref[q], NN)
    values = jnp.sum(acc, axis=0, keepdims=True)
    val_ref[...] = values
    row8 = lax.broadcasted_iota(jnp.int32, (GR, HD), 0)
    lane8 = lax.broadcasted_iota(jnp.int32, (GR, HD), 1)
    means = jnp.zeros((GR, HD), jnp.float32)
    for j in range(SEQ_DEV):
        total = jnp.sum(share_ref[j : j + 1, :] * values, axis=1, keepdims=True)
        mean = jnp.broadcast_to(total, (GR, HD))
        high = mean.astype(jnp.bfloat16).astype(jnp.float32)
        middle = (mean - high).astype(jnp.bfloat16).astype(jnp.float32)
        low = mean - high - middle
        term = jnp.where(row8 == QPK, high, jnp.where(row8 == QPK + 1, middle, low))
        means = jnp.where((lane8 == SEQ_DEV * place + j) & (row8 >= QPK), term, means)
    resid = jnp.where(mask_ref[...] == 1, values - target_ref[...], 0.0) * grad_scale
    r_high, r_low = split(resid)
    both = jnp.concatenate(
        [jnp.broadcast_to(r_high, (HROWS, rows)), jnp.broadcast_to(r_low, (HROWS, rows))], axis=0
    )
    acc = jnp.zeros((2 * HROWS, rows), jnp.float32)
    for q in range(QH):
        own = (q // QPK) * GR + q % QPK
        acc = acc + dot(jnp.where(row64 == own, both, zero64), p_ref[q], NT)
    c2 = jnp.concatenate(split(acc[0:HROWS] + acc[HROWS:]), axis=0)
    g2 = dot(c2, x_ref[...], NN)
    gt_ref[...] = g2[0:HROWS] + g2[HROWS:]
    for k in range(n // 4):
        tiles = [gt_ref[:, (5 * k + q) * HD : (5 * k + q + 1) * HD] for q in range(5)]
        for r in range(4):
            main = tiles[r]
            if r:
                main = jnp.where(group32 < 4 - r, turn(tiles[r], -TAIL * r), turn(tiles[r + 1], -TAIL * r))
            tail = pack_tail([tiles[r + 1][g * GR : (g + 1) * GR] for g in range(KVH)], r) + means
            i = 4 * k + r
            out_ref[i % across, i // across] = jnp.concatenate([main, tail], axis=0).astype(jnp.bfloat16)


def seen_kernel(x_ref, own_ref, out_ref):
    out_ref[...] = x_ref[0:GR, 0:HD].astype(jnp.float32)


def line_kernel(in_ref, out_ref):
    low = AXES["zl"]
    for h in range(AXES["zh"]):
        total = jnp.sum(in_ref[:, h].astype(jnp.float32), axis=0).astype(jnp.bfloat16)
        for i in range(low):
            out_ref[h * low + i] = total


def group_kernel(in_ref, out_ref):
    total = jnp.sum(in_ref[...].astype(jnp.float32), axis=0).astype(jnp.bfloat16)
    for i in range(out_ref.shape[0]):
        out_ref[i] = total


def seq_kernel(plan_ref, in_ref, own_ref, seq_ref, val_ref):
    val_ref[...] = own_ref[...]
    mine = lax.axis_index("zl")
    block = jnp.zeros((GR, HD), jnp.float32)
    for h in range(AXES["zh"]):
        block = block + in_ref[h * AXES["zl"] + mine, HROWS:PROWS, :].astype(jnp.float32)
    row8 = lax.broadcasted_iota(jnp.int32, (GR, HD), 0)
    mean = jnp.sum(jnp.where(row8 >= QPK, block, 0.0), axis=0, keepdims=True)
    slot = lax.broadcasted_iota(jnp.int32, (1, HD), 1)
    lane = lax.broadcasted_iota(jnp.int32, (1, SEQ_DEV), 1)
    out = jnp.zeros((1, SEQ_DEV), jnp.float32)
    for i in range(SEQ_DEV):
        own = jnp.sum(jnp.where(slot == plan_ref[0, i], mean, 0.0), axis=1, keepdims=True)
        out = jnp.where(lane == i, own, out)
    seq_ref[...] = out


def weight_kernel(head_ref, in_ref, out_ref):
    total = jnp.sum(in_ref[...].astype(jnp.float32), axis=0)
    main = total[0:HROWS]
    tail = jnp.concatenate([turn(total[HROWS:PROWS], -TAIL * g) for g in range(KVH)], axis=0)
    main2 = jnp.concatenate(split(main), axis=0)
    tail2 = jnp.concatenate(split(tail), axis=0)
    for g in range(KVH):
        head = head_rows(head_ref, g).astype(jnp.bfloat16)
        blank = jnp.zeros((GR, HD), jnp.bfloat16)
        block = jnp.concatenate([head if i == g else blank for i in range(KVH)] * 2, axis=0)
        cols = slice(g * HD, (g + 1) * HD)
        out_ref[0:HD, cols] = dot(main2, block, TN).astype(jnp.bfloat16)
        out_ref[HD:PIECE, cols] = dot(tail2, block, TN)[0:TAIL].astype(jnp.bfloat16)


def local(hidden, queries, keys, value_weight, value_head, lengths, plan, targets, loss_mask):
    n = math.prod(AXES[a] for a in FSDP)
    groups = math.prod(AXES[a] for a in DP)
    rows, d = hidden.shape[1:]
    grad_scale = 1.0 / math.sqrt(rows * n * groups)
    bf16, f32 = jnp.bfloat16, jnp.float32
    smem = pl.BlockSpec(memory_space=pltpu.SMEM)
    vmem = pl.BlockSpec(memory_space=pltpu.VMEM)
    own_lengths = lengths.reshape(1, SEQ_DEV)

    folded = pl.pallas_call(
        fold_kernel,
        out_shape=jax.ShapeDtypeStruct((n // 2, PROWS, HD), bf16),
        compiler_params=WIDE,
        name="fold",
    )(value_weight, value_head)
    own_core = lax.all_to_all(folded, ("zh", "x"), 0, 0)
    probs, share = pl.pallas_call(
        probs_kernel,
        grid=(KVH,),
        in_specs=[
            smem,
            pl.BlockSpec((rows, QPK * HD), lambda g: (0, g)),
            pl.BlockSpec((rows, HD), lambda g: (0, g)),
        ],
        out_specs=[
            pl.BlockSpec((QPK, rows, rows), lambda g: (g, 0, 0)),
            pl.BlockSpec((GR, rows), lambda g: (0, 0)),
        ],
        out_shape=[jax.ShapeDtypeStruct((QH, rows, rows), bf16), jax.ShapeDtypeStruct((GR, rows), f32)],
        scratch_shapes=[pltpu.VMEM((rows, rows), f32)],
        compiler_params=WIDE,
        cost_estimate=pl.CostEstimate(
            flops=2 * QH * rows * rows * HD, bytes_accessed=6 * 2**20, transcendentals=QH * rows * rows
        ),
        name="probs",
    )(own_lengths, queries[0], keys[0])

    own_core, probs = lax.optimization_barrier((own_core, probs))
    other_core = lax.ppermute(own_core, "core", [(0, 1), (1, 0)])

    seen = pl.pallas_call(
        seen_kernel,
        in_specs=[vmem, pl.BlockSpec(memory_space=pl.ANY)],
        out_shape=jax.ShapeDtypeStruct((GR, HD), f32),
        compiler_params=VMEM,
        cost_estimate=pl.CostEstimate(flops=0, bytes_accessed=4 * 2**20, transcendentals=0),
        name="seen",
    )(hidden[0], own_core)

    own_values, pieces = pl.pallas_call(
        functools.partial(main_kernel, grad_scale),
        in_specs=[pl.BlockSpec(memory_space=pl.ANY)] + [vmem] * 7,
        out_shape=[
            jax.ShapeDtypeStruct((1, rows), f32),
            jax.ShapeDtypeStruct((n // AXES["zh"], AXES["zh"], PROWS, HD), bf16),
        ],
        scratch_shapes=[pltpu.VMEM((HROWS, d), bf16), pltpu.VMEM((HROWS, d), f32)],
        compiler_params=VMEM,
        name="main",
    )(seen, share, own_core, other_core, hidden[0], probs, targets, loss_mask)
    terms = lax.all_to_all(pieces, ("x", "core"), 0, 0)

    line = pl.pallas_call(
        line_kernel,
        out_shape=jax.ShapeDtypeStruct((AXES["zh"] * AXES["zl"], PROWS, HD), bf16),
        compiler_params=VMEM,
        name="line",
    )(terms)
    lines = lax.all_to_all(line, ("zh", "zl"), 0, 0)

    copies = pl.pallas_call(
        group_kernel,
        out_shape=jax.ShapeDtypeStruct((AXES["y"], PROWS, HD), bf16),
        compiler_params=VMEM,
        name="group",
    )(lines)
    sums = lax.all_to_all(copies, "y", 0, 0)

    seq_values, values = pl.pallas_call(
        seq_kernel,
        in_specs=[smem, vmem, vmem],
        out_shape=[jax.ShapeDtypeStruct((1, SEQ_DEV), f32), jax.ShapeDtypeStruct((1, rows), f32)],
        compiler_params=VMEM,
        cost_estimate=pl.CostEstimate(flops=2**20, bytes_accessed=2**20, transcendentals=0),
        name="seq",
    )(plan, lines, own_values)

    d_weight = pl.pallas_call(
        weight_kernel,
        out_shape=jax.ShapeDtypeStruct(value_weight.shape, bf16),
        compiler_params=VMEM,
        name="weight",
    )(value_head, sums)
    return values, seq_values, d_weight


def solution(mesh):
    fine = Mesh(mesh.devices.reshape(tuple(AXES.values())), tuple(AXES))
    in_specs = (
        P(DP, FSDP, None),
        P(DP, FSDP, None),
        P(DP, FSDP, None),
        P(FSDP, None),
        P(),
        P(DP, FSDP, None),
        P(DP, FSDP),
        P(DP, FSDP),
        P(DP, FSDP),
    )
    out_specs = (P(DP, FSDP), P(DP, FSDP), P(FSDP, None))
    return jax.shard_map(local, mesh=fine, in_specs=in_specs, out_specs=out_specs, check_vma=False)
```

```python
import functools
import math

import jax
import jax.numpy as jnp
from jax import lax
from jax.experimental import pallas as pl
from jax.experimental.pallas import tpu as pltpu
from jax.sharding import Mesh
from jax.sharding import PartitionSpec as P

KVH = 4
QPK = 5
QH = KVH * QPK
HD = 128
SEQ_DEV = 4
AXES = {"zh": 4, "x": 4, "core": 2, "y": 8, "zl": 3}
FSDP = ("zh", "x", "core")
DP = ("y", "zl")
GR = 8
QR = 24
PIECE = 160
PROWS = QR + GR
BOTH = QR + KVH * GR
TAIL = 32

NT = (((1,), (1,)), ((), ()))
NN = (((1,), (0,)), ((), ()))
TN = (((0,), (0,)), ((), ()))
VMEM = pltpu.CompilerParams(vmem_limit_bytes=24 * 1024 * 1024)
WIDE = pltpu.CompilerParams(vmem_limit_bytes=60 * 1024 * 1024)


def dot(a, b, dims):
    return lax.dot_general(a, b, dims, preferred_element_type=jnp.float32)


def two_terms(x):
    high = x.astype(jnp.bfloat16).astype(jnp.float32)
    return jnp.concatenate([high, x - high], axis=0).astype(jnp.bfloat16)


def lane_group(rows):
    return lax.broadcasted_iota(jnp.int32, (rows, HD), 1) // TAIL


def turn(x, shift):
    shift = shift % HD
    return x if shift == 0 else pltpu.roll(x, shift, 1)


def head_rows(head_ref, rows, first, count):
    row = lax.broadcasted_iota(jnp.int32, (rows, HD), 0)
    out = jnp.zeros((rows, HD), jnp.float32)
    for p in range(count):
        q = first + p
        line = head_ref[q * HD : (q + 1) * HD].astype(jnp.float32).reshape(1, HD)
        out = jnp.where(row == p, jnp.broadcast_to(line, (rows, HD)), out)
    return out


def heads_of(all_heads, g):
    row = lax.broadcasted_iota(jnp.int32, all_heads.shape, 0)
    return jnp.where((row >= g * QPK) & (row < (g + 1) * QPK), all_heads, 0.0).astype(jnp.bfloat16)


def pack_tail(parts, r):
    group = lane_group(GR)
    tail = jnp.zeros((GR, HD), jnp.float32)
    for g in range(KVH):
        tail = jnp.where(group == g, turn(parts[g], TAIL * (g - r)), tail)
    return tail


def rows_of(q, rows):
    row = lax.broadcasted_iota(jnp.int32, (BOTH, rows), 0)
    return (row == q) | (row == QR + (q // QPK) * GR + q % QPK)


def fold_kernel(w_ref, head_ref, out_ref):
    n = out_ref.shape[0]
    all_heads = head_rows(head_ref, QR, 0, QH)
    main = jnp.zeros((QR, HD), jnp.float32)
    tails = []
    for g in range(KVH):
        cols = slice(g * HD, (g + 1) * HD)
        main = main + dot(heads_of(all_heads, g), w_ref[0:HD, cols], NT)
        own = head_rows(head_ref, GR, g * QPK, QPK).astype(jnp.bfloat16)
        tails.append(dot(own, w_ref[PIECE - HD : PIECE, cols], NT))
    packed = jnp.concatenate([main, pack_tail(tails, 3)], axis=0).astype(jnp.bfloat16)
    for i in range(n):
        out_ref[i] = packed


def probs_kernel(len_ref, q_ref, k_ref, out_ref, share_ref, bias_ref):
    rows = k_ref.shape[0]

    @pl.when(pl.program_id(0) == 0)
    def _():
        s = lax.broadcasted_iota(jnp.int32, (rows, rows), 0)
        t = lax.broadcasted_iota(jnp.int32, (rows, rows), 1)
        start = jnp.zeros((rows, rows), jnp.int32)
        end = 0
        for j in range(SEQ_DEV - 1):
            end = end + len_ref[0, j]
            start = jnp.where(t >= end, end, start)
        bias_ref[...] = jnp.where((s <= t) & (s >= start), 0.0, -jnp.inf)
        row = lax.broadcasted_iota(jnp.int32, (GR, rows), 0)
        pos = lax.broadcasted_iota(jnp.int32, (GR, rows), 1)
        share = jnp.zeros((GR, rows), jnp.float32)
        begin = 0
        for j in range(SEQ_DEV):
            size = len_ref[0, j]
            hit = (row == j) & (pos >= begin) & (pos < begin + size)
            share = jnp.where(hit, 1.0 / (jnp.zeros((GR, rows), jnp.float32) + size.astype(jnp.float32)), share)
            begin = begin + size
        share_ref[...] = share

    bias = bias_ref[...]
    scale = math.log2(math.e) / math.sqrt(HD)
    for p in range(QPK):
        score = dot(k_ref[...], q_ref[:, p * HD : (p + 1) * HD], NT) + bias
        top = jnp.max(score, axis=0, keepdims=True)
        expo = jnp.exp2((score - top) * scale)
        total = jnp.sum(expo, axis=0, keepdims=True)
        out_ref[p] = (expo * (1.0 / total)).astype(jnp.bfloat16)


def main_kernel(
    grad_scale, seen_ref, share_ref, own_ref, other_ref, x_ref, p_ref, target_ref, mask_ref, val_ref, out_ref, wht_ref, gt_ref
):
    n = 2 * own_ref.shape[0]
    across, depth = out_ref.shape[:2]
    rows = x_ref.shape[0]
    group24, group32 = lane_group(QR), lane_group(KVH * GR)
    core = lax.axis_index("core")
    place = (lax.axis_index("zh") * AXES["x"] + lax.axis_index("x")) * AXES["core"] + core

    def piece(i, part):
        own, other = own_ref[i // 2, part, :].astype(jnp.float32), other_ref[i // 2, part, :].astype(jnp.float32)
        return jnp.where(core == i % 2, own, other)

    for k in range(n // 4):
        main = [piece(4 * k + r, slice(0, QR)) for r in range(4)]
        tail = [piece(4 * k + r, slice(QR, PROWS)) for r in range(4)]
        for q in range(5):
            tile = jnp.zeros((QR, HD), jnp.float32)
            tails = jnp.zeros((KVH * GR, HD), jnp.float32)
            if q < 4:
                tile = jnp.where(group24 >= q, turn(main[q], TAIL * q), tile)
            if q >= 1:
                r = q - 1
                tile = jnp.where(group24 < r, turn(main[r], TAIL * r), tile)
                moved = jnp.concatenate([turn(tail[r], TAIL * (r - g)) for g in range(KVH)], axis=0)
                tails = jnp.where(group32 == r, moved, tails)
            j = 5 * k + q
            wht_ref[:, j * HD : (j + 1) * HD] = jnp.concatenate([tile, tails], axis=0).astype(jnp.bfloat16)
    u = dot(wht_ref[...], x_ref[...], NT).astype(jnp.bfloat16)
    zero = jnp.zeros((BOTH, rows), jnp.bfloat16)
    acc = jnp.zeros((BOTH, rows), jnp.float32)
    for q in range(QH):
        acc = acc + dot(jnp.where(rows_of(q, rows), u, zero), p_ref[q], NN)
    values = jnp.sum(acc, axis=0, keepdims=True)
    val_ref[...] = values
    row8 = lax.broadcasted_iota(jnp.int32, (GR, HD), 0)
    lane8 = lax.broadcasted_iota(jnp.int32, (GR, HD), 1)
    means = jnp.zeros((GR, HD), jnp.float32)
    for j in range(SEQ_DEV):
        total = jnp.sum(share_ref[j : j + 1, :] * values, axis=1, keepdims=True)
        mean = jnp.broadcast_to(total, (GR, HD))
        high = mean.astype(jnp.bfloat16).astype(jnp.float32)
        middle = (mean - high).astype(jnp.bfloat16).astype(jnp.float32)
        low = mean - high - middle
        term = jnp.where(row8 == QPK, high, jnp.where(row8 == QPK + 1, middle, low))
        means = jnp.where((lane8 == SEQ_DEV * place + j) & (row8 >= QPK), term, means)
    resid = jnp.where(mask_ref[...] == 1, values - target_ref[...], 0.0) * grad_scale
    every = jnp.broadcast_to(resid, (BOTH, rows)).astype(jnp.bfloat16)
    acc = jnp.zeros((BOTH, rows), jnp.float32)
    for q in range(QH):
        acc = acc + dot(jnp.where(rows_of(q, rows), every, zero), p_ref[q], NT)
    gt_ref[...] = dot(acc.astype(jnp.bfloat16), x_ref[...], NN)
    for k in range(n // 4):
        tiles = [gt_ref[0:QR, (5 * k + q) * HD : (5 * k + q + 1) * HD] for q in range(5)]
        for r in range(4):
            main = tiles[r]
            if r:
                main = jnp.where(group24 < 4 - r, turn(tiles[r], -TAIL * r), turn(tiles[r + 1], -TAIL * r))
            cols = slice((5 * k + r + 1) * HD, (5 * k + r + 2) * HD)
            tail = pack_tail([gt_ref[QR + g * GR : QR + (g + 1) * GR, cols] for g in range(KVH)], r) + means
            i = 4 * k + r
            out_ref[i % across, i // across] = jnp.concatenate([main, tail], axis=0).astype(jnp.bfloat16)


def seen_kernel(x_ref, own_ref, out_ref):
    out_ref[...] = x_ref[0:GR, 0:HD].astype(jnp.float32)


def line_kernel(in_ref, out_ref):
    low = AXES["zl"]
    for h in range(AXES["zh"]):
        total = jnp.sum(in_ref[:, h].astype(jnp.float32), axis=0).astype(jnp.bfloat16)
        for i in range(low):
            out_ref[h * low + i] = total


def group_kernel(in_ref, out_ref):
    total = jnp.sum(in_ref[...].astype(jnp.float32), axis=0).astype(jnp.bfloat16)
    for i in range(out_ref.shape[0]):
        out_ref[i] = total


def last_kernel(plan_ref, line_ref, own_ref, head_ref, in_ref, seq_ref, val_ref, out_ref):
    val_ref[...] = own_ref[...]
    mine = lax.axis_index("zl")
    block = jnp.zeros((GR, HD), jnp.float32)
    for h in range(AXES["zh"]):
        block = block + line_ref[h * AXES["zl"] + mine, QR:PROWS, :].astype(jnp.float32)
    row8 = lax.broadcasted_iota(jnp.int32, (GR, HD), 0)
    mean = jnp.sum(jnp.where(row8 >= QPK, block, 0.0), axis=0, keepdims=True)
    slot = lax.broadcasted_iota(jnp.int32, (1, HD), 1)
    lane = lax.broadcasted_iota(jnp.int32, (1, SEQ_DEV), 1)
    out = jnp.zeros((1, SEQ_DEV), jnp.float32)
    for i in range(SEQ_DEV):
        own = jnp.sum(jnp.where(slot == plan_ref[0, i], mean, 0.0), axis=1, keepdims=True)
        out = jnp.where(lane == i, own, out)
    seq_ref[...] = out

    total = jnp.sum(in_ref[...].astype(jnp.float32), axis=0)
    main2 = two_terms(total[0:QR])
    all_heads = head_rows(head_ref, QR, 0, QH)
    for g in range(KVH):
        cols = slice(g * HD, (g + 1) * HD)
        wide = heads_of(all_heads, g).astype(jnp.float32)
        wide2 = jnp.concatenate([wide, wide], axis=0).astype(jnp.bfloat16)
        out_ref[0:HD, cols] = dot(main2, wide2, TN).astype(jnp.bfloat16)
        small = head_rows(head_ref, GR, g * QPK, QPK)
        small2 = jnp.concatenate([small, small], axis=0).astype(jnp.bfloat16)
        tail2 = two_terms(turn(total[QR:PROWS], -TAIL * g))
        out_ref[HD:PIECE, cols] = dot(tail2, small2, TN)[0:TAIL].astype(jnp.bfloat16)


def local(hidden, queries, keys, value_weight, value_head, lengths, plan, targets, loss_mask):
    n = math.prod(AXES[a] for a in FSDP)
    groups = math.prod(AXES[a] for a in DP)
    rows, d = hidden.shape[1:]
    grad_scale = 1.0 / math.sqrt(rows * n * groups)
    bf16, f32 = jnp.bfloat16, jnp.float32
    smem = pl.BlockSpec(memory_space=pltpu.SMEM)
    vmem = pl.BlockSpec(memory_space=pltpu.VMEM)
    own_lengths = lengths.reshape(1, SEQ_DEV)

    folded = pl.pallas_call(
        fold_kernel,
        out_shape=jax.ShapeDtypeStruct((n // 2, PROWS, HD), bf16),
        compiler_params=WIDE,
        name="fold",
    )(value_weight, value_head)
    own_core = lax.all_to_all(folded, ("zh", "x"), 0, 0)
    probs, share = pl.pallas_call(
        probs_kernel,
        grid=(KVH,),
        in_specs=[
            smem,
            pl.BlockSpec((rows, QPK * HD), lambda g: (0, g)),
            pl.BlockSpec((rows, HD), lambda g: (0, g)),
        ],
        out_specs=[
            pl.BlockSpec((QPK, rows, rows), lambda g: (g, 0, 0)),
            pl.BlockSpec((GR, rows), lambda g: (0, 0)),
        ],
        out_shape=[jax.ShapeDtypeStruct((QH, rows, rows), bf16), jax.ShapeDtypeStruct((GR, rows), f32)],
        scratch_shapes=[pltpu.VMEM((rows, rows), f32)],
        compiler_params=WIDE,
        cost_estimate=pl.CostEstimate(
            flops=2 * QH * rows * rows * HD, bytes_accessed=6 * 2**20, transcendentals=QH * rows * rows
        ),
        name="probs",
    )(own_lengths, queries[0], keys[0])

    own_core, probs = lax.optimization_barrier((own_core, probs))
    other_core = lax.ppermute(own_core, "core", [(0, 1), (1, 0)])

    seen = pl.pallas_call(
        seen_kernel,
        in_specs=[vmem, pl.BlockSpec(memory_space=pl.ANY)],
        out_shape=jax.ShapeDtypeStruct((GR, HD), f32),
        compiler_params=VMEM,
        cost_estimate=pl.CostEstimate(flops=0, bytes_accessed=4 * 2**20, transcendentals=0),
        name="seen",
    )(hidden[0], own_core)

    own_values, pieces = pl.pallas_call(
        functools.partial(main_kernel, grad_scale),
        in_specs=[pl.BlockSpec(memory_space=pl.ANY)] + [vmem] * 7,
        out_shape=[
            jax.ShapeDtypeStruct((1, rows), f32),
            jax.ShapeDtypeStruct((n // AXES["zh"], AXES["zh"], PROWS, HD), bf16),
        ],
        scratch_shapes=[pltpu.VMEM((BOTH, d), bf16), pltpu.VMEM((BOTH, d), f32)],
        compiler_params=VMEM,
        name="main",
    )(seen, share, own_core, other_core, hidden[0], probs, targets, loss_mask)
    terms = lax.all_to_all(pieces, ("x", "core"), 0, 0)

    line = pl.pallas_call(
        line_kernel,
        out_shape=jax.ShapeDtypeStruct((AXES["zh"] * AXES["zl"], PROWS, HD), bf16),
        compiler_params=VMEM,
        name="line",
    )(terms)
    lines = lax.all_to_all(line, ("zh", "zl"), 0, 0)

    copies = pl.pallas_call(
        group_kernel,
        out_shape=jax.ShapeDtypeStruct((AXES["y"], PROWS, HD), bf16),
        compiler_params=VMEM,
        name="group",
    )(lines)
    sums = lax.all_to_all(copies, "y", 0, 0)

    seq_values, values, d_weight = pl.pallas_call(
        last_kernel,
        in_specs=[smem] + [vmem] * 4,
        out_shape=[
            jax.ShapeDtypeStruct((1, SEQ_DEV), f32),
            jax.ShapeDtypeStruct((1, rows), f32),
            jax.ShapeDtypeStruct(value_weight.shape, bf16),
        ],
        compiler_params=VMEM,
        name="last",
    )(plan, lines, own_values, value_head, sums)
    return values, seq_values, d_weight


def solution(mesh):
    fine = Mesh(mesh.devices.reshape(tuple(AXES.values())), tuple(AXES))
    in_specs = (
        P(DP, FSDP, None),
        P(DP, FSDP, None),
        P(DP, FSDP, None),
        P(FSDP, None),
        P(),
        P(DP, FSDP, None),
        P(DP, FSDP),
        P(DP, FSDP),
        P(DP, FSDP),
    )
    out_specs = (P(DP, FSDP), P(DP, FSDP), P(FSDP, None))
    return jax.shard_map(local, mesh=fine, in_specs=in_specs, out_specs=out_specs, check_vma=False)
```

```python
import functools
import math

import jax
import jax.numpy as jnp
from jax import lax
from jax.experimental import pallas as pl
from jax.experimental.pallas import tpu as pltpu
from jax.sharding import Mesh
from jax.sharding import PartitionSpec as P

KVH = 4
QPK = 5
QH = KVH * QPK
HD = 128
SEQ_DEV = 4
AXES = {"zh": 4, "x": 4, "core": 2, "y": 8, "zl": 3}
FSDP = ("zh", "x", "core")
DP = ("y", "zl")
GR = 8
QR = 24
PIECE = 160
PROWS = QR + GR
BOTH = QR + KVH * GR
TAIL = 32

NT = (((1,), (1,)), ((), ()))
NN = (((1,), (0,)), ((), ()))
TN = (((0,), (0,)), ((), ()))
VMEM = pltpu.CompilerParams(vmem_limit_bytes=24 * 1024 * 1024)
WIDE = pltpu.CompilerParams(vmem_limit_bytes=60 * 1024 * 1024)


def dot(a, b, dims):
    return lax.dot_general(a, b, dims, preferred_element_type=jnp.float32)


def two_terms(x):
    high = x.astype(jnp.bfloat16).astype(jnp.float32)
    return jnp.concatenate([high, x - high], axis=0).astype(jnp.bfloat16)


def lane_group(rows):
    return lax.broadcasted_iota(jnp.int32, (rows, HD), 1) // TAIL


def turn(x, shift):
    shift = shift % HD
    return x if shift == 0 else pltpu.roll(x, shift, 1)


def head_rows(head_ref, rows, first, count):
    row = lax.broadcasted_iota(jnp.int32, (rows, HD), 0)
    out = jnp.zeros((rows, HD), jnp.float32)
    for p in range(count):
        q = first + p
        line = head_ref[q * HD : (q + 1) * HD].astype(jnp.float32).reshape(1, HD)
        out = jnp.where(row == p, jnp.broadcast_to(line, (rows, HD)), out)
    return out


def heads_of(all_heads, g):
    row = lax.broadcasted_iota(jnp.int32, all_heads.shape, 0)
    return jnp.where((row >= g * QPK) & (row < (g + 1) * QPK), all_heads, 0.0).astype(jnp.bfloat16)


def pack_tail(parts, r):
    group = lane_group(GR)
    tail = jnp.zeros((GR, HD), jnp.float32)
    for g in range(KVH):
        tail = jnp.where(group == g, turn(parts[g], TAIL * (g - r)), tail)
    return tail


def rows_of(q, rows):
    row = lax.broadcasted_iota(jnp.int32, (BOTH, rows), 0)
    return (row == q) | (row == QR + (q // QPK) * GR + q % QPK)


def fold_kernel(w_ref, head_ref, out_ref):
    n = out_ref.shape[0]
    all_heads = head_rows(head_ref, QR, 0, QH)
    main = jnp.zeros((QR, HD), jnp.float32)
    tails = []
    for g in range(KVH):
        cols = slice(g * HD, (g + 1) * HD)
        main = main + dot(heads_of(all_heads, g), w_ref[0:HD, cols], NT)
        own = head_rows(head_ref, GR, g * QPK, QPK).astype(jnp.bfloat16)
        tails.append(dot(own, w_ref[PIECE - HD : PIECE, cols], NT))
    packed = jnp.concatenate([main, pack_tail(tails, 3)], axis=0).astype(jnp.bfloat16)
    for i in range(n):
        out_ref[i] = packed


def probs_kernel(len_ref, q_ref, k_ref, out_ref, share_ref, bias_ref):
    rows = k_ref.shape[0]

    @pl.when(pl.program_id(0) == 0)
    def _():
        s = lax.broadcasted_iota(jnp.int32, (rows, rows), 0)
        t = lax.broadcasted_iota(jnp.int32, (rows, rows), 1)
        start = jnp.zeros((rows, rows), jnp.int32)
        end = 0
        for j in range(SEQ_DEV - 1):
            end = end + len_ref[0, j]
            start = jnp.where(t >= end, end, start)
        bias_ref[...] = jnp.where((s <= t) & (s >= start), 0.0, -jnp.inf)
        row = lax.broadcasted_iota(jnp.int32, (GR, rows), 0)
        pos = lax.broadcasted_iota(jnp.int32, (GR, rows), 1)
        share = jnp.zeros((GR, rows), jnp.float32)
        begin = 0
        for j in range(SEQ_DEV):
            size = len_ref[0, j]
            hit = (row == j) & (pos >= begin) & (pos < begin + size)
            share = jnp.where(hit, 1.0 / (jnp.zeros((GR, rows), jnp.float32) + size.astype(jnp.float32)), share)
            begin = begin + size
        share_ref[...] = share

    scale = math.log2(math.e) / math.sqrt(HD)
    half = rows // 2
    for p in range(QPK):
        for t, s in ((slice(0, half), slice(0, half)), (slice(half, rows), slice(0, rows))):
            score = dot(k_ref[s, :], q_ref[t, p * HD : (p + 1) * HD], NT) + bias_ref[s, t]
            top = jnp.max(score, axis=0, keepdims=True)
            expo = jnp.exp2((score - top) * scale)
            total = jnp.sum(expo, axis=0, keepdims=True)
            out_ref[p, s, t] = (expo * (1.0 / total)).astype(jnp.bfloat16)
        out_ref[p, half:rows, 0:half] = jnp.zeros((half, half), jnp.bfloat16)


def main_kernel(
    grad_scale, seen_ref, share_ref, own_ref, other_ref, x_ref, p_ref, target_ref, mask_ref, val_ref, out_ref, wht_ref, gt_ref
):
    n = 2 * own_ref.shape[0]
    across, depth = out_ref.shape[:2]
    rows = x_ref.shape[0]
    group24, group32 = lane_group(QR), lane_group(KVH * GR)
    core = lax.axis_index("core")
    place = (lax.axis_index("zh") * AXES["x"] + lax.axis_index("x")) * AXES["core"] + core

    def piece(i, part):
        own, other = own_ref[i // 2, part, :].astype(jnp.float32), other_ref[i // 2, part, :].astype(jnp.float32)
        return jnp.where(core == i % 2, own, other)

    for k in range(n // 4):
        main = [piece(4 * k + r, slice(0, QR)) for r in range(4)]
        tail = [piece(4 * k + r, slice(QR, PROWS)) for r in range(4)]
        for q in range(5):
            tile = jnp.zeros((QR, HD), jnp.float32)
            tails = jnp.zeros((KVH * GR, HD), jnp.float32)
            if q < 4:
                tile = jnp.where(group24 >= q, turn(main[q], TAIL * q), tile)
            if q >= 1:
                r = q - 1
                tile = jnp.where(group24 < r, turn(main[r], TAIL * r), tile)
                moved = jnp.concatenate([turn(tail[r], TAIL * (r - g)) for g in range(KVH)], axis=0)
                tails = jnp.where(group32 == r, moved, tails)
            j = 5 * k + q
            wht_ref[:, j * HD : (j + 1) * HD] = jnp.concatenate([tile, tails], axis=0).astype(jnp.bfloat16)
    u = dot(wht_ref[...], x_ref[...], NT).astype(jnp.bfloat16)
    zero = jnp.zeros((BOTH, rows), jnp.bfloat16)
    acc = jnp.zeros((BOTH, rows), jnp.float32)
    for q in range(QH):
        acc = acc + dot(jnp.where(rows_of(q, rows), u, zero), p_ref[q], NN)
    values = jnp.sum(acc, axis=0, keepdims=True)
    val_ref[...] = values
    row8 = lax.broadcasted_iota(jnp.int32, (GR, HD), 0)
    lane8 = lax.broadcasted_iota(jnp.int32, (GR, HD), 1)
    means = jnp.zeros((GR, HD), jnp.float32)
    for j in range(SEQ_DEV):
        total = jnp.sum(share_ref[j : j + 1, :] * values, axis=1, keepdims=True)
        mean = jnp.broadcast_to(total, (GR, HD))
        high = mean.astype(jnp.bfloat16).astype(jnp.float32)
        middle = (mean - high).astype(jnp.bfloat16).astype(jnp.float32)
        low = mean - high - middle
        term = jnp.where(row8 == QPK, high, jnp.where(row8 == QPK + 1, middle, low))
        means = jnp.where((lane8 == SEQ_DEV * place + j) & (row8 >= QPK), term, means)
    resid = jnp.where(mask_ref[...] == 1, values - target_ref[...], 0.0) * grad_scale
    every = jnp.broadcast_to(resid, (BOTH, rows)).astype(jnp.bfloat16)
    acc = jnp.zeros((BOTH, rows), jnp.float32)
    for q in range(QH):
        acc = acc + dot(jnp.where(rows_of(q, rows), every, zero), p_ref[q], NT)
    gt_ref[...] = dot(acc.astype(jnp.bfloat16), x_ref[...], NN)
    for k in range(n // 4):
        tiles = [gt_ref[0:QR, (5 * k + q) * HD : (5 * k + q + 1) * HD] for q in range(5)]
        for r in range(4):
            main = tiles[r]
            if r:
                main = jnp.where(group24 < 4 - r, turn(tiles[r], -TAIL * r), turn(tiles[r + 1], -TAIL * r))
            cols = slice((5 * k + r + 1) * HD, (5 * k + r + 2) * HD)
            tail = pack_tail([gt_ref[QR + g * GR : QR + (g + 1) * GR, cols] for g in range(KVH)], r) + means
            i = 4 * k + r
            out_ref[i % across, i // across] = jnp.concatenate([main, tail], axis=0).astype(jnp.bfloat16)


def seen_kernel(x_ref, own_ref, out_ref):
    out_ref[...] = x_ref[0:GR, 0:HD].astype(jnp.float32)


def line_kernel(in_ref, out_ref):
    low = AXES["zl"]
    for h in range(AXES["zh"]):
        total = jnp.sum(in_ref[:, h].astype(jnp.float32), axis=0).astype(jnp.bfloat16)
        for i in range(low):
            out_ref[h * low + i] = total


def group_kernel(in_ref, out_ref):
    total = jnp.sum(in_ref[...].astype(jnp.float32), axis=0).astype(jnp.bfloat16)
    for i in range(out_ref.shape[0]):
        out_ref[i] = total


def last_kernel(plan_ref, line_ref, own_ref, head_ref, in_ref, seq_ref, val_ref, out_ref):
    val_ref[...] = own_ref[...]
    mine = lax.axis_index("zl")
    block = jnp.zeros((GR, HD), jnp.float32)
    for h in range(AXES["zh"]):
        block = block + line_ref[h * AXES["zl"] + mine, QR:PROWS, :].astype(jnp.float32)
    row8 = lax.broadcasted_iota(jnp.int32, (GR, HD), 0)
    mean = jnp.sum(jnp.where(row8 >= QPK, block, 0.0), axis=0, keepdims=True)
    slot = lax.broadcasted_iota(jnp.int32, (1, HD), 1)
    lane = lax.broadcasted_iota(jnp.int32, (1, SEQ_DEV), 1)
    out = jnp.zeros((1, SEQ_DEV), jnp.float32)
    for i in range(SEQ_DEV):
        own = jnp.sum(jnp.where(slot == plan_ref[0:1, i : i + 1], mean, 0.0), axis=1, keepdims=True)
        out = jnp.where(lane == i, own, out)
    seq_ref[...] = out

    total = jnp.sum(in_ref[...].astype(jnp.float32), axis=0)
    main2 = two_terms(total[0:QR])
    all_heads = head_rows(head_ref, QR, 0, QH)
    for g in range(KVH):
        cols = slice(g * HD, (g + 1) * HD)
        wide = heads_of(all_heads, g).astype(jnp.float32)
        wide2 = jnp.concatenate([wide, wide], axis=0).astype(jnp.bfloat16)
        out_ref[0:HD, cols] = dot(main2, wide2, TN).astype(jnp.bfloat16)
        small = head_rows(head_ref, GR, g * QPK, QPK)
        small2 = jnp.concatenate([small, small], axis=0).astype(jnp.bfloat16)
        tail2 = two_terms(turn(total[QR:PROWS], -TAIL * g))
        out_ref[HD:PIECE, cols] = dot(tail2, small2, TN)[0:TAIL].astype(jnp.bfloat16)


def local(hidden, queries, keys, value_weight, value_head, lengths, plan, targets, loss_mask):
    n = math.prod(AXES[a] for a in FSDP)
    groups = math.prod(AXES[a] for a in DP)
    rows, d = hidden.shape[1:]
    grad_scale = 1.0 / math.sqrt(rows * n * groups)
    bf16, f32 = jnp.bfloat16, jnp.float32
    smem = pl.BlockSpec(memory_space=pltpu.SMEM)
    vmem = pl.BlockSpec(memory_space=pltpu.VMEM)
    own_lengths = lengths.reshape(1, SEQ_DEV)

    folded = pl.pallas_call(
        fold_kernel,
        out_shape=jax.ShapeDtypeStruct((n // 2, PROWS, HD), bf16),
        compiler_params=WIDE,
        name="fold",
    )(value_weight, value_head)
    own_core = lax.all_to_all(folded, ("zh", "x"), 0, 0)
    probs, share = pl.pallas_call(
        probs_kernel,
        grid=(KVH,),
        in_specs=[
            smem,
            pl.BlockSpec((rows, QPK * HD), lambda g: (0, g)),
            pl.BlockSpec((rows, HD), lambda g: (0, g)),
        ],
        out_specs=[
            pl.BlockSpec((QPK, rows, rows), lambda g: (g, 0, 0)),
            pl.BlockSpec((GR, rows), lambda g: (0, 0)),
        ],
        out_shape=[jax.ShapeDtypeStruct((QH, rows, rows), bf16), jax.ShapeDtypeStruct((GR, rows), f32)],
        scratch_shapes=[pltpu.VMEM((rows, rows), f32)],
        compiler_params=WIDE,
        cost_estimate=pl.CostEstimate(
            flops=2 * QH * rows * rows * HD, bytes_accessed=6 * 2**20, transcendentals=QH * rows * rows
        ),
        name="probs",
    )(own_lengths, queries[0], keys[0])

    own_core, probs = lax.optimization_barrier((own_core, probs))
    other_core = lax.ppermute(own_core, "core", [(0, 1), (1, 0)])

    seen = pl.pallas_call(
        seen_kernel,
        in_specs=[vmem, pl.BlockSpec(memory_space=pl.ANY)],
        out_shape=jax.ShapeDtypeStruct((GR, HD), f32),
        compiler_params=VMEM,
        cost_estimate=pl.CostEstimate(flops=0, bytes_accessed=4 * 2**20, transcendentals=0),
        name="seen",
    )(hidden[0], own_core)

    own_values, pieces = pl.pallas_call(
        functools.partial(main_kernel, grad_scale),
        in_specs=[pl.BlockSpec(memory_space=pl.ANY)] + [vmem] * 7,
        out_shape=[
            jax.ShapeDtypeStruct((1, rows), f32),
            jax.ShapeDtypeStruct((n // AXES["zh"], AXES["zh"], PROWS, HD), bf16),
        ],
        scratch_shapes=[pltpu.VMEM((BOTH, d), bf16), pltpu.VMEM((BOTH, d), f32)],
        compiler_params=VMEM,
        name="main",
    )(seen, share, own_core, other_core, hidden[0], probs, targets, loss_mask)
    terms = lax.all_to_all(pieces, ("x", "core"), 0, 0)

    line = pl.pallas_call(
        line_kernel,
        out_shape=jax.ShapeDtypeStruct((AXES["zh"] * AXES["zl"], PROWS, HD), bf16),
        compiler_params=VMEM,
        name="line",
    )(terms)
    lines = lax.all_to_all(line, ("zh", "zl"), 0, 0)

    copies = pl.pallas_call(
        group_kernel,
        out_shape=jax.ShapeDtypeStruct((AXES["y"], PROWS, HD), bf16),
        compiler_params=VMEM,
        name="group",
    )(lines)
    sums = lax.all_to_all(copies, "y", 0, 0)

    seq_values, values, d_weight = pl.pallas_call(
        last_kernel,
        in_specs=[vmem] * 5,
        out_shape=[
            jax.ShapeDtypeStruct((1, SEQ_DEV), f32),
            jax.ShapeDtypeStruct((1, rows), f32),
            jax.ShapeDtypeStruct(value_weight.shape, bf16),
        ],
        compiler_params=VMEM,
        name="last",
    )(plan, lines, own_values, value_head, sums)
    return values, seq_values, d_weight


def solution(mesh):
    fine = Mesh(mesh.devices.reshape(tuple(AXES.values())), tuple(AXES))
    in_specs = (
        P(DP, FSDP, None),
        P(DP, FSDP, None),
        P(DP, FSDP, None),
        P(FSDP, None),
        P(),
        P(DP, FSDP, None),
        P(DP, FSDP),
        P(DP, FSDP),
        P(DP, FSDP),
    )
    out_specs = (P(DP, FSDP), P(DP, FSDP), P(FSDP, None))
    return jax.shard_map(local, mesh=fine, in_specs=in_specs, out_specs=out_specs, check_vma=False)
```
